32 devices in a mesh: row: 8 (over z, x), col: 4 (over y, core).
Axes of the slice: x: 2, y: 2, z: 4, core: 2. Of those that a mesh axis runs over, the one named last changes fastest.
Arguments:
- inverse_tiles: bfloat16 [16384, 16384], P('row', 'col'), may hold values from -0.046875 to 0.046875
- factor: bfloat16 [16384, 4, 512], P('row', None, 'col'), may hold values from -0.75 to 0.75
- inverse_diag: float32 [4, 512, 512], P(None, 'row', 'col'), may hold values from -6 to 6
- tile_list: int32 [4, 128], replicated, may hold values from 0 to 127, as said below
- tile_count: int32 [4], replicated, may hold values from 86 to 128, as said below
Outputs:
- inverse_panel: bfloat16 [16384, 4, 512], P(('row', 'col'))
- diag_block: float32 [4, 512, 512], P(None, 'row', 'col')
The draws below stay inside these ranges and needn't reach their ends.
Inputs may be any that keep to these rules, and one draw needn't show every extreme that they name: For each supernode the first tile_count entries of tile_list name distinct tiles in increasing order; the remaining entries name the tiles that are not listed. `tile_count`: some supernode lists all 128 tiles.
All inputs are finite; a program needn't handle non-finite values.
Results may differ from the reference program's by a relative error of at most 0.014.
Values may be sent and summed in bfloat16 or wider, within the bound.
No kernel may reach another device: no remote copies, remote signals or barrier semaphores. Data moves between devices by JAX's collectives and lax.ppermute only.
A program may use at most 128 MiB of HBM per device.

```python
import jax
import jax.numpy as jnp
from jax import lax

NS = 4
W = 512
TILE = 128
NA = 16384
NT = 128


def listed_tiles(key):
    base = jax.random.fold_in(key, 7)
    key_pick, key_drop, key_perm = jax.random.split(base, 3)
    complete = jax.random.randint(key_pick, (), 0, NS)
    dropped = jax.random.randint(key_drop, (NS,), 0, NT // 3 + 1)
    dropped = jnp.where(jnp.arange(NS) == complete, 0, dropped)
    counts = (NT - dropped).astype(jnp.int32)
    shuffled = jax.vmap(lambda one_key: jax.random.permutation(one_key, NT))(jax.random.split(key_perm, NS))
    position = jnp.arange(NT, dtype=jnp.int32)[None, :]
    ordering = jnp.where(position < counts[:, None], shuffled, shuffled + NT)
    ordered = jnp.sort(ordering, axis=1)
    ordered = jnp.where(ordered >= NT, ordered - NT, ordered)
    return (ordered.astype(jnp.int32), counts)


def draw_tile_list(key, part):
    return listed_tiles(key)[0]


def draw_tile_count(key, part):
    return listed_tiles(key)[1]


def shard_levels(own_key, shape, cuts, smallest, largest):
    def one(axis_at, parts):
        draws = jax.random.uniform(jax.random.fold_in(jax.random.fold_in(own_key, 6), axis_at), (parts,), jnp.float32, smallest / len(cuts), largest / len(cuts))
        return jnp.repeat(jnp.exp(draws), shape[axis_at] // parts).reshape((-1,) + (1,) * (len(shape) - axis_at - 1))

    loudness = one(*cuts[0])
    for cut in cuts[1:]:
        loudness = loudness * one(*cut)
    return loudness


def bell_draw(stream_key, extent, width, reach, cuts=(), kind=jnp.bfloat16):
    values = jax.random.normal(stream_key, extent, jnp.float32) * width
    if len(cuts) > 0:
        values = shard_levels(stream_key, extent, cuts, -0.22, 0.18) * values
    return jnp.clip(values, min=-reach, max=reach).astype(kind)


def setup_inputs(seed: int = 0) -> dict:
    key_of = jax.random.split(jax.random.key(seed), 6)
    inverse_tiles = bell_draw(key_of[0], (NA, NA), NA ** -0.5, 0.046875, ((0, 8), (1, 4)))
    factor = bell_draw(key_of[1], (NA, NS, W), 64 ** -0.5, 0.75, ((0, 8), (2, 4)))
    inverse_diag = bell_draw(key_of[2], (NS, W, W), 1.0, 6.0, ((1, 8), (2, 4)), jnp.float32)
    tile_list = draw_tile_list(jax.random.fold_in(key_of[5], 71), 0)
    tile_count = draw_tile_count(jax.random.fold_in(key_of[5], 71), 0)
    return {"inverse_tiles": inverse_tiles, "factor": factor, "inverse_diag": inverse_diag, "tile_list": tile_list, "tile_count": tile_count}


def listed_rows(tile_list, tile_count):
    tile_total = tile_list.shape[1]
    position = jnp.arange(tile_total, dtype=jnp.int32)
    matches = (tile_list[:, :, None] == position[None, None, :]) & (position[None, :, None] < tile_count[:, None, None])
    listed = jnp.any(matches, axis=1).astype(jnp.float32)
    return jnp.repeat(listed, TILE, axis=1)


def reference(inverse_tiles, factor, inverse_diag, tile_list, tile_count):
    row_live = listed_rows(tile_list, tile_count).T
    masked = jnp.where(row_live[:, :, None] > 0, factor, jnp.zeros_like(factor))
    product = jnp.dot(inverse_tiles, masked.reshape(NA, NS * W), preferred_element_type=jnp.float32)
    panel_full = -product.reshape(NA, NS, W) * row_live[:, :, None]
    diag_term = jnp.einsum("rsv,rsw->svw", masked.astype(jnp.float32), panel_full, precision=lax.Precision.HIGHEST)
    return panel_full.astype(jnp.bfloat16), inverse_diag - diag_term
```

```python
import functools

import jax
import jax.numpy as jnp
from jax import lax
from jax.experimental import pallas as pl
from jax.experimental.pallas import tpu as pltpu
from jax.sharding import PartitionSpec as P

TILE = 128
AXES = ("row", "col")
LANES = 128


class Grid:
    def __init__(self, rows, cols):
        self.rows, self.cols = rows, cols
        self.per = rows // cols

    def move(self, value, target):
        pairs = []
        for i in range(self.rows):
            for j in range(self.cols):
                to = target(i, j)
                if to is not None:
                    pairs.append((i * self.cols + j, to[0] * self.cols + to[1]))
        return lax.ppermute(value, AXES, pairs)

    def col_swap(self, value, bits):
        return self.move(value, lambda i, j: (i, j ^ bits))

    def row_swap(self, value, bits):
        return self.move(value, lambda i, j: (i ^ bits, j))

    def group_shift(self, value, step, held=0):
        def target(i, j):
            group = i // self.per
            source, to = group - held, group + step
            if 0 <= source < self.cols and 0 <= to < self.cols:
                return (i + step * self.per, j)
            return None

        return self.move(value, target)


def line_gather(grid, own):
    n = grid.cols
    values = {0: own}
    for sign in (1, -1):
        for far in range(1, n):
            if far <= 2:
                values[sign * far] = grid.group_shift(own, sign * far)
            else:
                values[sign * far] = grid.group_shift(
                    values[sign * (far - 1)], sign, held=sign * (far - 1)
                )
    return [values[delta] for delta in range(-(n - 1), n)]


def pick_kernel(n, where_ref, *refs):
    values, outs, sems = refs[: 2 * n - 1], refs[2 * n - 1 : 3 * n - 1], refs[3 * n - 1]
    for d in range(n):
        for k in range(2 * n - 1):

            @pl.when(where_ref[d] == k)
            def _(d=d, k=k):
                pltpu.make_async_copy(values[k], outs[d], sems.at[d]).start()

    for d in range(n):
        pltpu.make_async_copy(values[0], outs[d], sems.at[d]).wait()


def pick(grid, values, where):
    n = grid.cols
    shape = values[0].shape
    if shape[-1] % LANES:
        stacked = jnp.stack(values)
        return [lax.dynamic_index_in_dim(stacked, where[d], 0, keepdims=False) for d in range(n)]
    size = values[0].size * 2
    return pl.pallas_call(
        functools.partial(pick_kernel, n),
        grid_spec=pltpu.PrefetchScalarGridSpec(
            num_scalar_prefetch=1,
            grid=(1,),
            in_specs=[pl.BlockSpec(memory_space=pl.ANY)] * (2 * n - 1),
            out_specs=[pl.BlockSpec(memory_space=pl.ANY)] * n,
            scratch_shapes=[pltpu.SemaphoreType.DMA((n,))],
        ),
        out_shape=[jax.ShapeDtypeStruct(shape, values[0].dtype)] * n,
        cost_estimate=pl.CostEstimate(flops=0, transcendentals=0, bytes_accessed=2 * n * size),
        name="pick",
    )(where, *values)


def panel_kernel(n, per, rows_all, where_ref, a_ref, *refs):
    pieces, refs = refs[: per * n], refs[per * n :]
    left, refs = refs[:n], refs[n:]
    keep, send, diag_keep, diag_send, right, diag, sems = refs
    col, offset, row = where_ref[0], where_ref[1], where_ref[2]
    width = pieces[0].shape[1]
    depth = pieces[0].shape[0]
    part = diag.shape[0] // rows_all
    step = pl.program_id(0)

    @pl.when(step == 0)
    def _():
        copies = []
        for t in range(per):
            for d in range(n):
                place = right.at[
                    pl.ds(pl.multiple_of((offset ^ t) * depth, depth), depth),
                    pl.ds(pl.multiple_of((col ^ d) * width, width), width),
                ]
                copies.append(pltpu.make_async_copy(pieces[t * n + d], place, sems.at[t * n + d]))
        for copy in copies:
            copy.start()
        diag[...] = jnp.zeros_like(diag)
        for copy in copies:
            copy.wait()

    product = jnp.dot(a_ref[...], right[...], preferred_element_type=jnp.float32)
    rounded = product.astype(jnp.bfloat16)

    @pl.when(step % 2 == 0)
    def _():
        keep[0] = product

    @pl.when(step % 2 == 1)
    def _():
        send[0] = rounded

    for d in range(n):
        at = pl.ds(pl.multiple_of((col ^ d) * width, width), width)
        diag[at, :] += lax.dot_general(
            left[d][0], rounded, (((0,), (0,)), ((), ())), preferred_element_type=jnp.float32
        )

    @pl.when(step == n - 1)
    def _():
        for d in range(n):
            at = pl.ds(pl.multiple_of((col ^ d) * width, width), width)
            for block in range(rows_all):
                value = diag[pl.ds(block * part, part), at]
                if d % 2 == 0:
                    diag_keep[d // 2, row ^ block] = value
                else:
                    diag_send[d // 2, row ^ block] = value.astype(jnp.bfloat16)


def panel(grid, where, inverse_tiles, pieces, left, supers):
    n, per, rows_all = grid.cols, grid.per, grid.rows
    col, offset, row = where[0], where[1], where[2]
    depth, width = pieces[0][0].shape[-2:]
    rows_blk, cols_blk = inverse_tiles.shape
    share = rows_blk // n
    panel_width = n * width
    part = panel_width // rows_all
    if width % LANES or len(supers) > 1:
        order_col = col ^ jnp.arange(n)
        order_off = offset ^ jnp.arange(per)
        order_row = row ^ jnp.arange(rows_all)
        right = jnp.stack([jnp.stack(line) for line in pieces])
        right = jnp.take(jnp.take(right, order_off, axis=0), order_col, axis=1)
        right = right.transpose(0, 3, 2, 1, 4).reshape(cols_blk, len(supers) * panel_width)
        product = jnp.dot(inverse_tiles, right, preferred_element_type=jnp.float32)
        product = product.reshape(rows_blk, len(supers), panel_width)
        own = jnp.take(jnp.stack([value[jnp.array(supers)] for value in left]), order_col, axis=0)
        diag = jnp.einsum(
            "dsrv,rsw->sdvw",
            own,
            product.astype(jnp.bfloat16),
            preferred_element_type=jnp.float32,
        )
        diag = diag.reshape(len(supers), rows_all, part, n, width).transpose(3, 1, 0, 2, 4)
        diag = jnp.take(jnp.take(diag, order_col, axis=0), order_row, axis=1)
        product = jnp.take(
            product.reshape(n, share, len(supers), panel_width), order_col, axis=0
        ).transpose(0, 2, 1, 3)
        return (
            product[0::2],
            product[1::2].astype(jnp.bfloat16),
            diag[0::2],
            diag[1::2].astype(jnp.bfloat16),
        )
    half = n // 2
    at = supers[0]
    return pl.pallas_call(
        functools.partial(panel_kernel, n, per, rows_all),
        grid_spec=pltpu.PrefetchScalarGridSpec(
            num_scalar_prefetch=1,
            grid=(n,),
            in_specs=[pl.BlockSpec((share, cols_blk), lambda d, w: (w[0] ^ d, 0))]
            + [pl.BlockSpec(memory_space=pl.ANY)] * (per * n)
            + [pl.BlockSpec((1, share, width), lambda d, w: (at, w[0] ^ d, 0))] * n,
            out_specs=[
                pl.BlockSpec((1, share, panel_width), lambda d, w: (d // 2, 0, 0)),
                pl.BlockSpec((1, share, panel_width), lambda d, w: (d // 2, 0, 0)),
                pl.BlockSpec((half, rows_all, part, width), lambda d, w: (0, 0, 0, 0)),
                pl.BlockSpec((half, rows_all, part, width), lambda d, w: (0, 0, 0, 0)),
            ],
            scratch_shapes=[
                pltpu.VMEM((cols_blk, panel_width), jnp.bfloat16),
                pltpu.VMEM((panel_width, panel_width), jnp.float32),
                pltpu.SemaphoreType.DMA((per * n,)),
            ],
        ),
        out_shape=[
            jax.ShapeDtypeStruct((half, share, panel_width), jnp.float32),
            jax.ShapeDtypeStruct((half, share, panel_width), jnp.bfloat16),
            jax.ShapeDtypeStruct((half, rows_all, part, width), jnp.float32),
            jax.ShapeDtypeStruct((half, rows_all, part, width), jnp.bfloat16),
        ],
        cost_estimate=pl.CostEstimate(
            flops=2 * rows_blk * panel_width * (cols_blk + panel_width),
            transcendentals=0,
            bytes_accessed=2 * rows_blk * cols_blk + 2 * panel_width * (cols_blk + rows_blk) + 3 * rows_blk * panel_width,
        ),
        name="panel",
    )(where, inverse_tiles, *[value for line in pieces for value in line], *left)


def halve_cols(grid, keep, send):
    bit = 1
    while True:
        keep = keep + grid.col_swap(send, bit).astype(jnp.float32)
        bit *= 2
        if bit >= grid.cols:
            return keep[0]
        send, keep = keep[1::2].astype(jnp.bfloat16), keep[0::2]


def halve_rows(grid, value):
    bit = 1
    while bit < grid.rows:
        send, value = value[1::2], value[0::2]
        value = value + grid.row_swap(send, bit)
        bit *= 2
    return value[0]


def per_device(inverse_tiles, factor, inverse_diag, tile_list, tile_count):
    grid = Grid(lax.axis_size("row"), lax.axis_size("col"))
    row = lax.axis_index("row")
    col = lax.axis_index("col")
    group, offset = row // grid.per, row % grid.per
    rows_blk, supers, width = factor.shape
    share = rows_blk // grid.cols
    tiles_blk = rows_blk // TILE

    position = jnp.arange(tile_list.shape[1], dtype=jnp.int32)
    mine = row * tiles_blk + jnp.arange(tiles_blk, dtype=jnp.int32)
    matches = (tile_list[:, None, :] == mine[None, :, None]) & (
        position[None, None, :] < tile_count[:, None, None]
    )
    listed = jnp.any(matches, axis=2)
    live = jnp.repeat(listed, TILE, axis=1)
    masked = jnp.where(
        live[:, :, None], factor.transpose(1, 0, 2), jnp.zeros((), factor.dtype)
    )

    together = 1 if width % LANES == 0 else supers
    chunks = [tuple(range(at, at + together)) for at in range(0, supers, together)]
    where_pick = group - (col ^ jnp.arange(grid.cols, dtype=jnp.int32)) + grid.cols - 1
    where_panel = jnp.stack([col, offset, row]).astype(jnp.int32)

    left = {0: masked}
    bit = grid.cols // 2
    while bit:
        for d in list(left):
            left[d | bit] = grid.col_swap(left[d], bit)
        bit //= 2
    left = [left[d] for d in range(grid.cols)]

    panels, diags = [], []
    for chunk in chunks:
        own = masked[chunk[0]] if len(chunk) == 1 else masked[chunk[0] : chunk[-1] + 1]
        picked = pick(grid, line_gather(grid, own), where_pick)
        line = [picked[0]] + [grid.col_swap(picked[d], d) for d in range(1, grid.cols)]
        pieces = [line] + [
            [grid.row_swap(value, t) for value in line] for t in range(1, grid.per)
        ]
        keep, send, diag_keep, diag_send = panel(
            grid, where_panel, inverse_tiles, pieces, left, chunk
        )
        total = halve_cols(grid, keep, send)
        diag = halve_rows(grid, halve_cols(grid, diag_keep, diag_send))
        panels.append(total.reshape(len(chunk), share, -1))
        diags.append(diag.reshape(len(chunk), -1, width))

    summed = jnp.concatenate(panels, axis=0)
    share_live = lax.dynamic_slice_in_dim(live, col * share, share, 1).astype(jnp.float32)
    inverse_panel = (-summed * share_live[:, :, None]).astype(jnp.bfloat16).transpose(1, 0, 2)
    diag_block = inverse_diag + jnp.concatenate(diags, axis=0)
    return (inverse_panel, diag_block)


def solution(mesh):
    placed = (P("row", "col"), P("row", None, "col"), P(None, "row", "col"), P(), P())
    return jax.shard_map(
        per_device,
        mesh=mesh,
        in_specs=placed,
        out_specs=(P(("row", "col"), None, None), P(None, "row", "col")),
        check_vma=False,
    )
```

```python
import functools

import jax
import jax.numpy as jnp
from jax import lax
from jax.experimental import pallas as pl
from jax.experimental.pallas import tpu as pltpu
from jax.sharding import PartitionSpec as P


TILE = 128
AXES = ("row", "col")
LANES = 128


class Grid:
    def __init__(self, rows, cols):
        self.rows, self.cols = rows, cols
        self.per = rows // cols

    def move(self, value, target):
        pairs = []
        for i in range(self.rows):
            for j in range(self.cols):
                to = target(i, j)
                if to is not None:
                    pairs.append((i * self.cols + j, to[0] * self.cols + to[1]))
        return lax.ppermute(value, AXES, pairs)

    def col_swap(self, value, bits):
        return self.move(value, lambda i, j: (i, j ^ bits))

    def row_swap(self, value, bits):
        return self.move(value, lambda i, j: (i ^ bits, j))

    def group_shift(self, value, step, held=0):
        def target(i, j):
            group = i // self.per
            source, to = group - held, group + step
            if 0 <= source < self.cols and 0 <= to < self.cols:
                return (i + step * self.per, j)
            return None

        return self.move(value, target)


def line_start(grid, own):
    values = {0: own}
    for far in (2, 1):
        for sign in (1, -1):
            if far < grid.cols:
                values[sign * far] = grid.group_shift(own, sign * far)
    return values


def line_finish(grid, values):
    for far in range(3, grid.cols):
        for sign in (1, -1):
            values[sign * far] = grid.group_shift(
                values[sign * (far - 1)], sign, held=sign * (far - 1)
            )
    return [values[delta] for delta in range(1 - grid.cols, grid.cols)]


def pick_kernel(n, where_ref, *refs):
    values, outs, sems = refs[: 2 * n - 1], refs[2 * n - 1 : 3 * n - 1], refs[3 * n - 1]
    for d in range(n):
        for k in range(2 * n - 1):

            @pl.when(where_ref[d] == k)
            def _(d=d, k=k):
                pltpu.make_async_copy(values[k], outs[d], sems.at[d]).start()

    for d in range(n):
        pltpu.make_async_copy(values[0], outs[d], sems.at[d]).wait()


def pick(grid, values, where):
    n = grid.cols
    shape = values[0].shape
    if shape[-1] % LANES:
        stacked = jnp.stack(values)
        return [lax.dynamic_index_in_dim(stacked, where[d], 0, keepdims=False) for d in range(n)]
    size = values[0].size * 2
    return pl.pallas_call(
        functools.partial(pick_kernel, n),
        grid_spec=pltpu.PrefetchScalarGridSpec(
            num_scalar_prefetch=1,
            grid=(1,),
            in_specs=[pl.BlockSpec(memory_space=pl.ANY)] * (2 * n - 1),
            out_specs=[pl.BlockSpec(shape, lambda g, w: (0,) * len(shape))] * n,
            scratch_shapes=[pltpu.SemaphoreType.DMA((n,))],
        ),
        out_shape=[jax.ShapeDtypeStruct(shape, values[0].dtype)] * n,
        cost_estimate=pl.CostEstimate(flops=0, transcendentals=0, bytes_accessed=2 * n * size),
        name="pick",
    )(where, *values)


def panel_kernel(n, per, rows_all, where_ref, a_ref, *refs):
    pieces, refs = refs[: per * n], refs[per * n :]
    left, refs = refs[:n], refs[n:]
    keep, send, diag_keep, diag_send, right, diag, sems = refs
    col, offset, row = where_ref[0], where_ref[1], where_ref[2]
    width = pieces[0].shape[1]
    depth = pieces[0].shape[0]
    part = diag.shape[0] // rows_all
    step = pl.program_id(0)

    @pl.when(step == 0)
    def _():
        copies = []
        for t in range(per):
            for d in range(n):
                place = right.at[
                    pl.ds(pl.multiple_of((offset ^ t) * depth, depth), depth),
                    pl.ds(pl.multiple_of((col ^ d) * width, width), width),
                ]
                copies.append(pltpu.make_async_copy(pieces[t * n + d], place, sems.at[t * n + d]))
        for copy in copies:
            copy.start()
        diag[...] = jnp.zeros_like(diag)
        for copy in copies:
            copy.wait()

    product = jnp.dot(a_ref[...], right[...], preferred_element_type=jnp.float32)
    rounded = product.astype(jnp.bfloat16)

    @pl.when(step % 2 == 0)
    def _():
        keep[0] = product

    @pl.when(step % 2 == 1)
    def _():
        send[0] = rounded

    for d in range(n):
        at = pl.ds(pl.multiple_of((col ^ d) * width, width), width)
        diag[at, :] += lax.dot_general(
            left[d][0], rounded, (((0,), (0,)), ((), ())), preferred_element_type=jnp.float32
        )

    @pl.when(step == n - 1)
    def _():
        for d in range(n):
            at = pl.ds(pl.multiple_of((col ^ d) * width, width), width)
            for block in range(rows_all):
                value = diag[pl.ds(block * part, part), at]
                if d % 2 == 0:
                    diag_keep[d // 2, row ^ block] = value
                else:
                    diag_send[d // 2, row ^ block] = value.astype(jnp.bfloat16)


def panel(grid, where, inverse_tiles, pieces, left, supers):
    n, per, rows_all = grid.cols, grid.per, grid.rows
    col, offset, row = where[0], where[1], where[2]
    _, width = pieces[0][0].shape[-2:]
    rows_blk, cols_blk = inverse_tiles.shape
    share = rows_blk // n
    panel_width = n * width
    part = panel_width // rows_all
    if width % LANES or len(supers) > 1:
        order_col = col ^ jnp.arange(n)
        order_off = offset ^ jnp.arange(per)
        order_row = row ^ jnp.arange(rows_all)
        right = jnp.stack([jnp.stack(line) for line in pieces])
        right = jnp.take(jnp.take(right, order_off, axis=0), order_col, axis=1)
        right = right.transpose(0, 3, 2, 1, 4).reshape(cols_blk, len(supers) * panel_width)
        product = jnp.dot(inverse_tiles, right, preferred_element_type=jnp.float32)
        product = product.reshape(rows_blk, len(supers), panel_width)
        own = jnp.take(jnp.stack([value[jnp.array(supers)] for value in left]), order_col, axis=0)
        diag = jnp.einsum(
            "dsrv,rsw->sdvw",
            own,
            product.astype(jnp.bfloat16),
            preferred_element_type=jnp.float32,
        )
        diag = diag.reshape(len(supers), rows_all, part, n, width).transpose(3, 1, 0, 2, 4)
        diag = jnp.take(jnp.take(diag, order_col, axis=0), order_row, axis=1)
        product = jnp.take(
            product.reshape(n, share, len(supers), panel_width), order_col, axis=0
        ).transpose(0, 2, 1, 3)
        return (
            product[0::2],
            product[1::2].astype(jnp.bfloat16),
            diag[0::2],
            diag[1::2].astype(jnp.bfloat16),
        )
    half = n // 2
    at = supers[0]
    return pl.pallas_call(
        functools.partial(panel_kernel, n, per, rows_all),
        grid_spec=pltpu.PrefetchScalarGridSpec(
            num_scalar_prefetch=1,
            grid=(n,),
            in_specs=[pl.BlockSpec((share, cols_blk), lambda d, w: (w[0] ^ d, 0))]
            + [pl.BlockSpec(memory_space=pl.ANY)] * (per * n)
            + [pl.BlockSpec((1, share, width), lambda d, w: (at, w[0] ^ d, 0))] * n,
            out_specs=[
                pl.BlockSpec((1, share, panel_width), lambda d, w: (d // 2, 0, 0)),
                pl.BlockSpec((1, share, panel_width), lambda d, w: (d // 2, 0, 0)),
                pl.BlockSpec((half, rows_all, part, width), lambda d, w: (0, 0, 0, 0)),
                pl.BlockSpec((half, rows_all, part, width), lambda d, w: (0, 0, 0, 0)),
            ],
            scratch_shapes=[
                pltpu.VMEM((cols_blk, panel_width), jnp.bfloat16),
                pltpu.VMEM((panel_width, panel_width), jnp.float32),
                pltpu.SemaphoreType.DMA((per * n,)),
            ],
        ),
        out_shape=[
            jax.ShapeDtypeStruct((half, share, panel_width), jnp.float32),
            jax.ShapeDtypeStruct((half, share, panel_width), jnp.bfloat16),
            jax.ShapeDtypeStruct((half, rows_all, part, width), jnp.float32),
            jax.ShapeDtypeStruct((half, rows_all, part, width), jnp.bfloat16),
        ],
        cost_estimate=pl.CostEstimate(
            flops=2 * rows_blk * panel_width * (cols_blk + panel_width),
            transcendentals=0,
            bytes_accessed=2 * rows_blk * cols_blk + 2 * panel_width * (cols_blk + rows_blk) + 3 * rows_blk * panel_width,
        ),
        name="panel",
    )(where, inverse_tiles, *[value for line in pieces for value in line], *left)


def reduce_panel(grid, keep, send, out):
    bit = 1
    while True:
        moved = grid.col_swap(send, bit)
        yield
        keep = keep + moved.astype(jnp.float32)
        bit *= 2
        if bit >= grid.cols:
            break
        send, keep = keep[1::2].astype(jnp.bfloat16), keep[0::2]
    out.append(keep[0])


def reduce_diag(grid, keep, send, out):
    yield from reduce_panel(grid, keep, send, out)
    value = out.pop()
    bit = 1
    while bit < grid.rows:
        moved = grid.row_swap(value[1::2], bit)
        yield
        value = value[0::2] + moved
        bit *= 2
    out.append(value[0])


def advance(running):
    for steps in list(running):
        if next(steps, running) is running:
            running.remove(steps)


def per_device(inverse_tiles, factor, inverse_diag, tile_list, tile_count):
    grid = Grid(lax.axis_size("row"), lax.axis_size("col"))
    row = lax.axis_index("row")
    col = lax.axis_index("col")
    group, offset = row // grid.per, row % grid.per
    rows_blk, supers, width = factor.shape
    share = rows_blk // grid.cols
    tiles_blk = rows_blk // TILE

    position = jnp.arange(tile_list.shape[1], dtype=jnp.int32)
    mine = row * tiles_blk + jnp.arange(tiles_blk, dtype=jnp.int32)
    matches = (tile_list[:, None, :] == mine[None, :, None]) & (
        position[None, None, :] < tile_count[:, None, None]
    )
    listed = jnp.any(matches, axis=2)
    live = jnp.repeat(listed, TILE, axis=1)
    masked = jnp.where(
        live[:, :, None], factor.transpose(1, 0, 2), jnp.zeros((), factor.dtype)
    )

    together = 1 if width % LANES == 0 else supers
    chunks = [tuple(range(at, at + together)) for at in range(0, supers, together)]
    where_pick = group - (col ^ jnp.arange(grid.cols, dtype=jnp.int32)) + grid.cols - 1
    where_panel = jnp.stack([col, offset, row]).astype(jnp.int32)

    def rows_of(chunk):
        return masked[chunk[0]] if len(chunk) == 1 else masked[chunk[0] : chunk[-1] + 1]

    last = len(chunks) - 1
    jobs = [(at, 0) for at in range(len(chunks))]
    if last:
        jobs += [(last, t) for t in range(1, grid.per)]
    lines, pieces, left = {}, {}, {0: masked}
    panels, diags = [[] for _ in chunks], [[] for _ in chunks]
    running = []

    def start(k):
        at, t = jobs[k]
        lines[k] = line_start(grid, early[t] if t else rows_of(chunks[at]))

    def spread(k):
        picked = pick(grid, lines.pop(k), where_pick)
        pieces[k] = [picked[0]] + [grid.col_swap(picked[d], d) for d in range(1, grid.cols)]

    def across(k, some):
        at, t = jobs[k]
        if last and at == last:
            return
        for t in range(1, grid.per):
            for d in some:
                pieces[k, t, d] = grid.row_swap(pieces[k][d], t)

    def multiply(at):
        if last and at == last:
            full = [pieces[k] for k in range(last, len(jobs))]
        else:
            full = [pieces[at]] + [
                [pieces[at, t, d] for d in range(grid.cols)] for t in range(1, grid.per)
            ]
        keep, send, diag_keep, diag_send = panel(
            grid, where_panel, inverse_tiles, full, [left[d] for d in range(grid.cols)], chunks[at]
        )
        running.append(reduce_diag(grid, diag_keep, diag_send, diags[at]))
        running.append(reduce_panel(grid, keep, send, panels[at]))

    start(0)
    bit = grid.cols // 2
    left[bit] = grid.col_swap(masked, bit)
    early = {}
    if last:
        early = {t: grid.row_swap(rows_of(chunks[last]), t) for t in range(1, grid.per)}
    bit //= 2
    near = [d for d in range(grid.cols) if d < 2]
    far = [d for d in range(grid.cols) if d >= 2]
    for k in range(len(jobs)):
        lines[k] = line_finish(grid, lines[k])
        if k + 1 < len(jobs):
            start(k + 1)
        if k:
            across(k - 1, far)
        advance(running)
        if k == len(jobs) - 1 and k >= 3:
            multiply(k - 3)
        spread(k)
        across(k, near)
        advance(running)
        if k == 0:
            while bit:
                for d in list(left):
                    left[d | bit] = grid.col_swap(left[d], bit)
                bit //= 2
        if 2 <= k < len(jobs) - 2 or (k >= 2 and k == len(jobs) - 2 and False):
            multiply(k - 2)
            advance(running)
    across(len(jobs) - 1, far)
    done = {at for at in range(len(chunks)) if 2 <= at + 2 < len(jobs) - 2}
    if len(jobs) >= 4:
        done.add(len(jobs) - 4)
    for at in range(len(chunks)):
        if at not in done:
            multiply(at)
            advance(running)
    while running:
        advance(running)
    panels = [value[0].reshape(len(chunk), share, -1) for value, chunk in zip(panels, chunks)]
    diags = [value[0].reshape(len(chunk), -1, width) for value, chunk in zip(diags, chunks)]

    summed = jnp.concatenate(panels, axis=0)
    share_live = lax.dynamic_slice_in_dim(live, col * share, share, 1).astype(jnp.float32)
    inverse_panel = (-summed * share_live[:, :, None]).astype(jnp.bfloat16).transpose(1, 0, 2)
    diag_block = inverse_diag + jnp.concatenate(diags, axis=0)
    return (inverse_panel, diag_block)


def solution(mesh):
    placed = (P("row", "col"), P("row", None, "col"), P(None, "row", "col"), P(), P())

    return jax.shard_map(
        per_device,
        mesh=mesh,
        in_specs=placed,
        out_specs=(P(("row", "col"), None, None), P(None, "row", "col")),
        check_vma=False,
    )
```

```python
import functools

import jax
import jax.numpy as jnp
from jax import lax
from jax.experimental import pallas as pl
from jax.experimental.pallas import tpu as pltpu
from jax.sharding import PartitionSpec as P


TILE = 128
AXES = ("row", "col")
LANES = 128


class Grid:
    def __init__(self, rows, cols):
        self.rows, self.cols = rows, cols
        self.per = rows // cols

    def move(self, value, target):
        pairs = []
        for i in range(self.rows):
            for j in range(self.cols):
                to = target(i, j)
                if to is not None:
                    pairs.append((i * self.cols + j, to[0] * self.cols + to[1]))
        return lax.ppermute(value, AXES, pairs)

    def col_swap(self, value, bits):
        return self.move(value, lambda i, j: (i, j ^ bits))

    def row_swap(self, value, bits):
        return self.move(value, lambda i, j: (i ^ bits, j))

    def group_swap(self, value, bits, some=None):
        def target(i, j):
            group = i // self.per
            if some is None or group in some:
                return ((group ^ bits) * self.per + i % self.per, j)
            return None

        return self.move(value, target)


def line_start(grid, own, relayed):
    if relayed:
        return [own, grid.group_swap(own, 2), grid.group_swap(own, 1), grid.group_swap(own, 3, (1, 2))]
    return [own] + [grid.group_swap(own, e) for e in range(grid.cols - 1, 0, -1)]


def line_finish(grid, values, relayed):
    if relayed:
        own, two, one, near = values
        return [own, one, two, near, grid.group_swap(two, 1, (1, 2))]
    return values[:1] + values[:0:-1]


def pick_kernel(n, m, where_ref, *refs):
    values, outs, sems = refs[:m], refs[m : m + n // 2], refs[m + n // 2]
    for d in range(n):
        for k in range(m):

            @pl.when(where_ref[d] == k)
            def _(d=d, k=k):
                pltpu.make_async_copy(values[k], outs[d // 2].at[d % 2], sems.at[d]).start()

    for d in range(n):
        pltpu.make_async_copy(values[0], outs[d // 2].at[d % 2], sems.at[d]).wait()


def pick(grid, values, where):
    n, m = grid.cols, len(values)
    shape = values[0].shape
    if shape[-1] % LANES:
        stacked = jnp.stack(values)
        return [jnp.take(stacked, where[d : d + 2], axis=0) for d in range(0, n, 2)]
    size = values[0].size * 2
    return pl.pallas_call(
        functools.partial(pick_kernel, n, m),
        grid_spec=pltpu.PrefetchScalarGridSpec(
            num_scalar_prefetch=1,
            grid=(1,),
            in_specs=[pl.BlockSpec(memory_space=pl.ANY)] * m,
            out_specs=[pl.BlockSpec((2,) + shape, lambda g, w: (0,) * (len(shape) + 1))] * (n // 2),
            scratch_shapes=[pltpu.SemaphoreType.DMA((n,))],
        ),
        out_shape=[jax.ShapeDtypeStruct((2,) + shape, values[0].dtype)] * (n // 2),
        cost_estimate=pl.CostEstimate(flops=0, transcendentals=0, bytes_accessed=2 * n * size),
        name="pick",
    )(where, *values)


def panel_kernel(n, per, rows_all, where_ref, a_ref, *refs):
    pieces, refs = refs[: per * n], refs[per * n :]
    left, refs = refs[:n], refs[n:]
    keep, send, diag_keep, diag_send, right, diag, sems = refs
    col, offset, row = where_ref[0], where_ref[1], where_ref[2]
    depth, width = pieces[0].shape[1:]
    part = diag.shape[0] // rows_all
    step = pl.program_id(0)

    @pl.when(step == 0)
    def _():
        copies = []
        for t in range(per):
            for d in range(n):
                place = right.at[
                    pl.ds(pl.multiple_of((offset ^ t) * depth, depth), depth),
                    pl.ds(pl.multiple_of((col ^ d) * width, width), width),
                ]
                copies.append(pltpu.make_async_copy(pieces[t * n + d].at[d % 2], place, sems.at[t * n + d]))
        for copy in copies:
            copy.start()
        diag[...] = jnp.zeros_like(diag)
        for copy in copies:
            copy.wait()

    product = jnp.dot(a_ref[...], right[...], preferred_element_type=jnp.float32)
    rounded = product.astype(jnp.bfloat16)

    @pl.when(step % 2 == 0)
    def _():
        keep[0] = product

    @pl.when(step % 2 == 1)
    def _():
        send[0] = rounded

    for d in range(n):
        at = pl.ds(pl.multiple_of((col ^ d) * width, width), width)
        diag[at, :] += lax.dot_general(
            left[d][0], rounded, (((0,), (0,)), ((), ())), preferred_element_type=jnp.float32
        )

    @pl.when(step == n - 1)
    def _():
        for d in range(n):
            at = pl.ds(pl.multiple_of((col ^ d) * width, width), width)
            for block in range(rows_all):
                value = diag[pl.ds(block * part, part), at]
                if d % 2 == 0:
                    diag_keep[d // 2, row ^ block] = value
                else:
                    diag_send[d // 2, row ^ block] = value.astype(jnp.bfloat16)


def panel(grid, where, inverse_tiles, pieces, left, supers):
    n, per, rows_all = grid.cols, grid.per, grid.rows
    col, offset, row = where[0], where[1], where[2]
    _, width = pieces[0][0].shape[-2:]
    rows_blk, cols_blk = inverse_tiles.shape
    share = rows_blk // n
    panel_width = n * width
    part = panel_width // rows_all
    if width % LANES or len(supers) > 1:
        order_col = col ^ jnp.arange(n)
        order_off = offset ^ jnp.arange(per)
        order_row = row ^ jnp.arange(rows_all)
        right = jnp.stack([jnp.stack([value[d % 2] for d, value in enumerate(line)]) for line in pieces])
        right = jnp.take(jnp.take(right, order_off, axis=0), order_col, axis=1)
        right = right.transpose(0, 3, 2, 1, 4).reshape(cols_blk, len(supers) * panel_width)
        product = jnp.dot(inverse_tiles, right, preferred_element_type=jnp.float32)
        product = product.reshape(rows_blk, len(supers), panel_width)
        own = jnp.take(jnp.stack([value[jnp.array(supers)] for value in left]), order_col, axis=0)
        diag = jnp.einsum(
            "dsrv,rsw->sdvw",
            own,
            product.astype(jnp.bfloat16),
            preferred_element_type=jnp.float32,
        )
        diag = diag.reshape(len(supers), rows_all, part, n, width).transpose(3, 1, 0, 2, 4)
        diag = jnp.take(jnp.take(diag, order_col, axis=0), order_row, axis=1)
        product = jnp.take(
            product.reshape(n, share, len(supers), panel_width), order_col, axis=0
        ).transpose(0, 2, 1, 3)
        return (
            product[0::2],
            product[1::2].astype(jnp.bfloat16),
            diag[0::2],
            diag[1::2].astype(jnp.bfloat16),
        )
    half = n // 2
    at = supers[0]
    return pl.pallas_call(
        functools.partial(panel_kernel, n, per, rows_all),
        grid_spec=pltpu.PrefetchScalarGridSpec(
            num_scalar_prefetch=1,
            grid=(n,),
            in_specs=[pl.BlockSpec((share, cols_blk), lambda d, w: (w[0] ^ d, 0))]
            + [pl.BlockSpec(memory_space=pl.ANY)] * (per * n)
            + [pl.BlockSpec((1, share, width), lambda d, w: (at, w[0] ^ d, 0))] * n,
            out_specs=[
                pl.BlockSpec((1, share, panel_width), lambda d, w: (d // 2, 0, 0)),
                pl.BlockSpec((1, share, panel_width), lambda d, w: (d // 2, 0, 0)),
                pl.BlockSpec((half, rows_all, part, width), lambda d, w: (0, 0, 0, 0)),
                pl.BlockSpec((half, rows_all, part, width), lambda d, w: (0, 0, 0, 0)),
            ],
            scratch_shapes=[
                pltpu.VMEM((cols_blk, panel_width), jnp.bfloat16),
                pltpu.VMEM((panel_width, panel_width), jnp.float32),
                pltpu.SemaphoreType.DMA((per * n,)),
            ],
        ),
        out_shape=[
            jax.ShapeDtypeStruct((half, share, panel_width), jnp.float32),
            jax.ShapeDtypeStruct((half, share, panel_width), jnp.bfloat16),
            jax.ShapeDtypeStruct((half, rows_all, part, width), jnp.float32),
            jax.ShapeDtypeStruct((half, rows_all, part, width), jnp.bfloat16),
        ],
        cost_estimate=pl.CostEstimate(
            flops=2 * rows_blk * panel_width * (cols_blk + panel_width),
            transcendentals=0,
            bytes_accessed=2 * rows_blk * cols_blk + 2 * panel_width * (cols_blk + rows_blk) + 3 * rows_blk * panel_width,
        ),
        name="panel",
    )(where, inverse_tiles, *[value for line in pieces for value in line], *left)


def reduce_panel(grid, keep, send, out):
    bit = 1
    while True:
        moved = grid.col_swap(send, bit)
        yield
        bit *= 2
        if bit >= grid.cols:
            break
        send = (keep[1::2] + moved[1::2].astype(jnp.float32)).astype(jnp.bfloat16)
        keep = keep[0::2] + moved[0::2].astype(jnp.float32)
    out.append(keep[0] + moved[0].astype(jnp.float32))


def reduce_rows(grid, value, out):
    bit = 1
    while bit < grid.rows:
        moved = grid.row_swap(value[1::2].astype(jnp.bfloat16), bit)
        yield
        value = value[0::2] + moved.astype(jnp.float32)
        bit *= 2
    out.append(value[0])


def advance(running):
    for steps in list(running):
        if next(steps, running) is running:
            running.remove(steps)


def per_device(inverse_tiles, factor, inverse_diag, tile_list, tile_count):
    grid = Grid(lax.axis_size("row"), lax.axis_size("col"))
    row = lax.axis_index("row")
    col = lax.axis_index("col")
    group, offset = row // grid.per, row % grid.per
    rows_blk, supers, width = factor.shape
    share = rows_blk // grid.cols
    tiles_blk = rows_blk // TILE

    position = jnp.arange(tile_list.shape[1], dtype=jnp.int32)
    mine = row * tiles_blk + jnp.arange(tiles_blk, dtype=jnp.int32)
    matches = (tile_list[:, None, :] == mine[None, :, None]) & (
        position[None, None, :] < tile_count[:, None, None]
    )
    listed = jnp.any(matches, axis=2)
    live = jnp.repeat(listed, TILE, axis=1)

    def mask(values, live):
        return jnp.where(live[..., None], values, jnp.zeros((), values.dtype))

    together = 1 if width % LANES == 0 else supers
    chunks = [tuple(range(at, at + together)) for at in range(0, supers, together)]
    if len(chunks) > 1:
        first = mask(factor[:, 0], live[0])
        first, factor = lax.optimization_barrier((first, factor))
    masked = mask(factor.transpose(1, 0, 2), live)
    if len(chunks) == 1:
        first = masked
    relayed = grid.cols == 4
    where_pick = group ^ col ^ jnp.arange(grid.cols, dtype=jnp.int32)
    where_relayed = where_pick + ((where_pick == 3) & ((group == 0) | (group == 3)))
    where_panel = jnp.stack([col, offset, row]).astype(jnp.int32)

    def rows_of(chunk):
        return masked[chunk[0]] if len(chunk) == 1 else masked[chunk[0] : chunk[-1] + 1]

    last = len(chunks) - 1
    jobs = [(at, 0) for at in range(len(chunks))]
    if last:
        jobs += [(last, t) for t in range(1, grid.per)]
    lines, pieces, left = {}, {}, {0: masked}
    panels, halves = [[] for _ in chunks], [[] for _ in chunks]
    ready, closed = set(), set()
    running = []
    pairs = range(grid.cols // 2)

    def through(k):
        return relayed and k < len(jobs) - 1

    def start(k):
        at, t = jobs[k]
        own = first if k == 0 else early[t] if t else rows_of(chunks[at])
        lines[k] = line_start(grid, own, through(k))

    def spread(k):
        picked = pick(grid, lines.pop(k), where_relayed if through(k) else where_pick)
        pieces[k] = [picked[0]] + [grid.col_swap(picked[p], 2 * p) for p in pairs[1:]]

    def across(k, some):
        at, t = jobs[k]
        if last and at == last:
            return
        for t in range(1, grid.per):
            for p in some:
                pieces[k, t, p] = grid.row_swap(pieces[k][p], t)

    def inner(values):
        return [value for pair in values for value in (pair, grid.col_swap(pair, 1))]

    def close(k):
        pieces[k] = inner(pieces[k])

    def close_across(k):
        at, t = jobs[k]
        if last and at == last:
            return
        for t in range(1, grid.per):
            pieces[k, t] = inner([pieces[k, t, p] for p in pairs])

    def multiply(at):
        if last and at == last:
            full = [pieces[k] for k in range(last, len(jobs))]
        else:
            full = [pieces[at]] + [pieces[at, t] for t in range(1, grid.per)]
        keep, send, diag_keep, diag_send = panel(
            grid, where_panel, inverse_tiles, full, [left[d] for d in range(grid.cols)], chunks[at]
        )
        running.append(reduce_panel(grid, diag_keep, diag_send, halves[at]))
        running.append(reduce_panel(grid, keep, send, panels[at]))
        advance(running)

    start(0)
    bit = grid.cols // 2
    left[bit] = grid.col_swap(masked, bit)
    early = {}
    if last:
        early = {t: grid.row_swap(rows_of(chunks[last]), t) for t in range(1, grid.per)}
    bit //= 2
    count = len(jobs)
    ahead = 1
    for k in range(count):
        if k not in ready:
            lines[k] = line_finish(grid, lines[k], through(k))
        if ahead == k + 1 < count:
            start(ahead)
            ahead += 1
        if k and k - 1 not in closed:
            across(k - 1, pairs[1:])
            close(k - 1)
        if 2 <= k < count - 2:
            close_across(k - 2)
        spread(k)
        across(k, pairs[:1])
        while bit:
            for d in list(left):
                left[d | bit] = grid.col_swap(left[d], bit)
            bit //= 2
        advance(running)
        if k == count - 3 > 0:
            start(ahead)
            ahead += 1
            multiply(k - 2)
            lines[k + 1] = line_finish(grid, lines[k + 1], through(k + 1))
            ready.add(k + 1)
            across(k, pairs[1:])
            close(k)
            closed.add(k)
        elif k == count - 2 > 1:
            close_across(k - 2)
            multiply(k - 2)
    across(count - 1, pairs[1:])
    rest = range(max(count - 3, 0), len(chunks))
    for at in rest:
        if at == rest[-1]:
            close(count - 1)
        close_across(at)
        multiply(at)
    while any(not half for half in halves):
        advance(running)
    diags = []
    value = jnp.stack([half[0] for half in halves], axis=1)
    running.insert(0, reduce_rows(grid, value, diags))
    while running:
        advance(running)
    panels = [value[0].reshape(len(chunk), share, -1) for value, chunk in zip(panels, chunks)]
    diag_block = inverse_diag + diags[0].reshape(inverse_diag.shape)
    summed = jnp.concatenate(panels, axis=0)
    share_live = lax.dynamic_slice_in_dim(live, col * share, share, 1).astype(jnp.float32)
    inverse_panel = (-summed * share_live[:, :, None]).astype(jnp.bfloat16).transpose(1, 0, 2)
    return (inverse_panel, diag_block)


def solution(mesh):
    placed = (P("row", "col"), P("row", None, "col"), P(None, "row", "col"), P(), P())

    return jax.shard_map(
        per_device,
        mesh=mesh,
        in_specs=placed,
        out_specs=(P(("row", "col"), None, None), P(None, "row", "col")),
        check_vma=False,
    )
```
